512 devices in a mesh: grp: 4 (over z_hi, core), wide: 128 (over z_lo, x, y).
Axes of the slice: x: 4, y: 8, z: 8 (z_hi: 2, z_lo: 4; z = z_hi * 4 + z_lo), core: 2. Of those that a mesh axis runs over, the one named last changes fastest.
Arguments:
- images: bfloat16 [2048, 256, 2048], P(('grp', 'wide')), may hold values from -6 to 6
- legendre_real: float32 [128, 128], replicated, may hold values from -0.375 to 0.375
- legendre_imag: float32 [128, 128], replicated, may hold values from -0.375 to 0.375
- amplitudes: float32 [128, 256, 128], P('wide'), may hold values from -6 to 6
Outputs:
- projected: float32 [128, 256, 128], P('wide', 'grp')
The draws below stay inside these ranges and needn't reach their ends.
All inputs are finite; a program needn't handle non-finite values.
Results may differ from the reference program's by a relative error of at most 0.0023.
Values may be sent and summed in bfloat16 or wider, within the bound.
No kernel may reach another device: no remote copies, remote signals or barrier semaphores. Data moves between devices by JAX's collectives and lax.ppermute only.
A program may use at most 64 MiB of HBM per device.

```python
import math
import jax
import jax.numpy as jnp
from jax import lax

RADII = 256
ANGLES = 2048
HARMS = 128
DEGREES = 128
MODELS = 128
IMAGES = 2048


def block_scale(rng, dims, shards, low, top_value):
    def one(axis_at, shards_of):
        steps = jax.random.uniform(jax.random.fold_in(jax.random.fold_in(rng, 6), axis_at), (shards_of,), jnp.float32, low / len(shards), top_value / len(shards))
        return jnp.repeat(jnp.exp(steps), dims[axis_at] // shards_of).reshape((-1,) + (1,) * (len(dims) - axis_at - 1))

    loudness = one(*shards[0])
    for cut in shards[1:]:
        loudness = loudness * one(*cut)
    return loudness


def noise(own_key, extent, width, bound, split=(), held_as=jnp.bfloat16):
    loudness = block_scale(own_key, extent, split, -0.22, 0.18) if split else 1.0
    entries = jax.random.normal(own_key, extent, jnp.float32) * width * loudness
    return jnp.minimum(jnp.maximum(entries, -bound), bound).astype(held_as)


def setup_inputs(seed: int = 0) -> dict:
    seeds = jax.random.split(jax.random.key(seed), 5)
    images = noise(seeds[0], (IMAGES, RADII, ANGLES), 1.0, 6.0, ((0, 512),))
    legendre_real = noise(seeds[1], (DEGREES, HARMS), (2 * HARMS) ** -0.5, 0.375, (), jnp.float32)
    legendre_imag = noise(seeds[2], (DEGREES, HARMS), (2 * HARMS) ** -0.5, 0.375, (), jnp.float32)
    amplitudes = noise(seeds[3], (DEGREES, RADII, MODELS), 1.0, 6.0, ((0, 128),), jnp.float32)
    return dict(images=images, legendre_real=legendre_real, legendre_imag=legendre_imag, amplitudes=amplitudes)


def harmonic_table(points, count):
    angle_idx = jnp.arange(points, dtype=jnp.int32)
    harm_idx = jnp.arange(count, dtype=jnp.int32)
    product = angle_idx[:, None] * harm_idx[None, :] % points
    phase = product.astype(jnp.float32) * (2.0 * math.pi / points)
    norm_scale = 1.0 / math.sqrt(points)
    both = jnp.concatenate([jnp.cos(phase) * norm_scale, -jnp.sin(phase) * norm_scale], axis=1)
    return both.astype(jnp.bfloat16)

def reference(images, legendre_real, legendre_imag, amplitudes):
    count_img = images.shape[0]
    table = harmonic_table(ANGLES, HARMS)
    spectra = jnp.dot(images.reshape(count_img * RADII, ANGLES), table, preferred_element_type=jnp.float32)
    spectra = spectra.astype(jnp.bfloat16).reshape(count_img, RADII, 2, HARMS)
    by_harm = jnp.moveaxis(spectra, 3, 0)

    def one_harm(block):
        values = block.astype(jnp.float32)
        gram = jnp.einsum('nra,nsb->abrs', values, values)
        real_part = (gram[0, 0] + gram[1, 1]) / count_img
        imag_part = (gram[1, 0] - gram[0, 1]) / count_img
        return jnp.stack([real_part, imag_part], axis=0)
    corr = lax.map(one_harm, by_harm)
    flat = corr.reshape(HARMS, 2, RADII * RADII)
    inverted = jnp.dot(legendre_real, flat[:, 0], precision=lax.Precision.HIGHEST)
    inverted = inverted + jnp.dot(legendre_imag, flat[:, 1], precision=lax.Precision.HIGHEST)
    inverted = inverted.reshape(DEGREES, RADII, RADII)
    return jnp.einsum('lrs,lsk->lrk', inverted, amplitudes, precision=lax.Precision.HIGHEST)
```

```python
import functools
import math

import jax
import jax.numpy as jnp
import ml_dtypes
import numpy as np
from jax import lax
from jax.experimental import pallas as pl
from jax.experimental.pallas import tpu as pltpu
from jax.sharding import PartitionSpec as P

HARMS = 128
LANES = 128


def table_rows(points, count):
    product = np.arange(count)[:, None] * np.arange(points)[None, :] % points
    phase = product.astype(np.float32) * np.float32(2.0 * math.pi / points)
    norm_scale = np.float32(1.0 / math.sqrt(points))
    both = np.concatenate([np.cos(phase) * norm_scale, -np.sin(phase) * norm_scale])
    return both.astype(ml_dtypes.bfloat16)


def spectra_kernel(img_ref, table_ref, out_ref, rows_ref):
    step = pl.program_id(0)
    count = pl.num_programs(0)
    harms = table_ref.shape[0] // 2
    both = lax.dot_general(
        table_ref[...], img_ref[0], (((1,), (1,)), ((), ())), preferred_element_type=jnp.float32
    )
    for lane in range(0, both.shape[1], LANES):
        cols = slice(lane, lane + LANES)
        rows_ref[lane // LANES, pl.ds(step, harms, stride=8), :] = both[:harms, cols]
        rows_ref[lane // LANES, pl.ds(step + 4, harms, stride=8), :] = both[harms:, cols]

    @pl.when(step == count - 1)
    def _():
        for half in range(rows_ref.shape[0]):
            out_ref[:, half * LANES:(half + 1) * LANES] = rows_ref[half].astype(jnp.bfloat16)


def spectra_call(images, table):
    count, radii, points = images.shape
    wide = table.shape[0]
    rows = wide * count
    return pl.pallas_call(
        spectra_kernel,
        grid=(count,),
        out_shape=jax.ShapeDtypeStruct((rows, radii), jnp.bfloat16),
        in_specs=[
            pl.BlockSpec((1, radii, points), lambda i: (i, 0, 0)),
            pl.BlockSpec((wide, points), lambda i: (0, 0), pipeline_mode=pl.Buffered(1)),
        ],
        out_specs=pl.BlockSpec((rows, radii), lambda i: (0, 0)),
        scratch_shapes=[pltpu.VMEM((radii // LANES, rows, LANES), jnp.float32)],
        name="spectra",
    )(images, table)


def gram_kernel(x_ref, own_ref, send_ref, gram_ref):
    core = lax.rem(lax.axis_index("grp"), 2)
    x = x_ref[...]
    rows, radii = x.shape
    wide = x.astype(jnp.float32).reshape(rows // 8, 8, radii)
    turned = pltpu.roll(wide, 4, 1)
    spot = lax.broadcasted_iota(jnp.int32, turned.shape, 1)
    turned = jnp.where(spot < 4, -turned, turned).reshape(rows, radii).astype(jnp.bfloat16)
    dims = (((0,), (0,)), ((), ()))
    gram_ref[:, :radii] = lax.dot_general(x, x, dims, preferred_element_type=jnp.float32)
    gram_ref[:, radii:] = lax.dot_general(x, turned, dims, preferred_element_type=jnp.float32)
    part = own_ref.shape[1]
    for top in range(2):
        mine = pl.multiple_of((2 * top + core) * part, 8)
        other = pl.multiple_of((2 * top + 1 - core) * part, 8)
        own_ref[top] = gram_ref[pl.ds(mine, part), :]
        send_ref[top] = gram_ref[pl.ds(other, part), :]


def gram_call(pooled):
    rows, radii = pooled.shape
    half = jax.ShapeDtypeStruct((2, radii // 4, 2 * radii), jnp.float32)
    return pl.pallas_call(
        gram_kernel,
        out_shape=(half, half),
        scratch_shapes=[pltpu.VMEM((radii, 2 * radii), jnp.float32)],
        name="gram",
    )(pooled)


def merge_kernel(scale, own_ref, got_ref, out_ref, rows_ref):
    radii = own_ref.shape[2] // 2
    part = own_ref.shape[1]
    for top in range(2):
        for half in range(2):
            for kind in range(2):
                cols = slice(kind * radii + half * LANES, kind * radii + (half + 1) * LANES)
                total = (own_ref[top, :, cols] + got_ref[top, :, cols]) * scale
                first = (top * 2 + half) * part * 2 + kind
                rows_ref[pl.ds(first, part, stride=2), :] = total
    out_ref[...] = rows_ref[...].astype(jnp.bfloat16)


def merge_call(own, got, total_img):
    rows = own.size // LANES
    return pl.pallas_call(
        functools.partial(merge_kernel, 1.0 / total_img),
        out_shape=jax.ShapeDtypeStruct((rows, LANES), jnp.bfloat16),
        scratch_shapes=[pltpu.VMEM((rows, LANES), jnp.float32)],
        name="merge",
    )(own, got)


def legendre_kernel(corr_ref, real_ref, imag_ref, out_ref, rows_ref):
    rows_ref[...] = corr_ref[...].astype(jnp.float32)
    harms = real_ref.shape[1]

    def summed(kind):
        low = rows_ref[pl.ds(kind, harms, stride=2), :]
        return low + rows_ref[pl.ds(2 * harms + kind, harms, stride=2), :]

    exact = functools.partial(
        jnp.dot, precision=lax.Precision.HIGHEST, preferred_element_type=jnp.float32
    )
    out_ref[...] = exact(real_ref[...], summed(0)) + exact(imag_ref[...], summed(1))


def legendre_call(corr, legendre_real, legendre_imag):
    degrees = legendre_real.shape[0]
    return pl.pallas_call(
        legendre_kernel,
        out_shape=jax.ShapeDtypeStruct((degrees, LANES), jnp.float32),
        scratch_shapes=[pltpu.VMEM(corr.shape, jnp.float32)],
        name="legendre",
    )(corr, legendre_real, legendre_imag)


def project_kernel(inv_ref, amp_ref, out_ref):
    part = inv_ref.shape[0] // 2
    exact = functools.partial(
        jnp.dot, precision=lax.Precision.HIGHEST, preferred_element_type=jnp.float32
    )
    low = exact(inv_ref[:part, :], amp_ref[0, :LANES, :])
    out_ref[0] = low + exact(inv_ref[part:, :], amp_ref[0, LANES:, :])


def project_call(inverted, amplitudes):
    return pl.pallas_call(
        project_kernel,
        out_shape=jax.ShapeDtypeStruct(
            (1, inverted.shape[0] // 2, amplitudes.shape[2]), jnp.float32
        ),
        name="project",
    )(inverted, amplitudes)


def body(images, legendre_real, legendre_imag, amplitudes):
    local_img, radii, points = images.shape
    groups = lax.axis_size("grp")
    owners = lax.axis_size("wide")
    total_img = local_img * groups * owners

    spectra = spectra_call(images, jnp.asarray(table_rows(points, HARMS)))
    spectra = spectra.reshape(HARMS, 2 * local_img, radii)
    pooled = lax.all_to_all(spectra, "wide", split_axis=0, concat_axis=0, tiled=True)

    own, send = gram_call(pooled.reshape(HARMS * 2 * local_img, radii))
    swap = [(g * owners + w, (g ^ 1) * owners + w) for g in range(groups) for w in range(owners)]
    got = lax.ppermute(send, ("grp", "wide"), swap)
    corr = merge_call(own, got, total_img)

    columns = [
        [(2 * top + core) * owners + w for top in range(2) for w in range(owners)]
        for core in range(2)
    ]
    every_harm = lax.all_to_all(
        corr.reshape(2 * owners, 2, LANES), ("grp", "wide"), split_axis=0, concat_axis=0,
        axis_index_groups=columns, tiled=True,
    )
    degree_part = legendre_call(
        every_harm.reshape(4 * owners, LANES), legendre_real, legendre_imag
    )
    mine = lax.all_to_all(
        degree_part.reshape(owners, 1, LANES), "wide", split_axis=0, concat_axis=0, tiled=True
    )
    return project_call(mine.reshape(owners, LANES), amplitudes)


def solution(mesh):
    return jax.shard_map(
        body,
        mesh=mesh,
        in_specs=(P(("grp", "wide"), None, None), P(), P(), P("wide", None, None)),
        out_specs=P("wide", "grp", None),
        check_vma=False,
    )
```

```python
import functools
import math

import jax
import jax.numpy as jnp
import ml_dtypes
import numpy as np
from jax import lax
from jax.experimental import pallas as pl
from jax.experimental.pallas import tpu as pltpu
from jax.sharding import PartitionSpec as P

HARMS = 128
LANES = 128


def table_rows(points, count):
    product = np.arange(count)[:, None] * np.arange(points)[None, :] % points
    phase = product.astype(np.float32) * np.float32(2.0 * math.pi / points)
    norm_scale = np.float32(1.0 / math.sqrt(points))
    both = np.concatenate([np.cos(phase) * norm_scale, -np.sin(phase) * norm_scale])
    return both.astype(ml_dtypes.bfloat16)


def spectra_kernel(img_hbm, table_hbm, out_ref, img_ref, table_ref, rows_ref, img_sem, table_sem):
    count = img_ref.shape[0]
    harms = table_ref.shape[0] // 2
    table_copy = pltpu.make_async_copy(table_hbm, table_ref, table_sem)
    table_copy.start()

    def image_copy(i):
        return pltpu.make_async_copy(img_hbm.at[i], img_ref.at[i], img_sem.at[i])

    @pl.loop(0, count)
    def _(i):
        image_copy(i).start()

    table_copy.wait()

    @pl.loop(0, count)
    def _(i):
        image_copy(i).wait()
        both = lax.dot_general(
            table_ref[...], img_ref[i], (((1,), (1,)), ((), ())), preferred_element_type=jnp.float32
        )
        for half in range(both.shape[1] // LANES):
            cols = slice(half * LANES, (half + 1) * LANES)
            rows_ref[half, pl.ds(i, harms, stride=8), :] = both[:harms, cols]
            rows_ref[half, pl.ds(i + 4, harms, stride=8), :] = both[harms:, cols]

    for half in range(rows_ref.shape[0]):
        out_ref[:, half * LANES:(half + 1) * LANES] = rows_ref[half].astype(jnp.bfloat16)


def spectra_call(images, table):
    count, radii, points = images.shape
    wide = table.shape[0]
    rows = wide * count
    return pl.pallas_call(
        spectra_kernel,
        out_shape=jax.ShapeDtypeStruct((rows, radii), jnp.bfloat16),
        in_specs=[pl.BlockSpec(memory_space=pltpu.HBM)] * 2,
        scratch_shapes=[
            pltpu.VMEM(images.shape, jnp.bfloat16),
            pltpu.VMEM(table.shape, jnp.bfloat16),
            pltpu.VMEM((radii // LANES, rows, LANES), jnp.float32),
            pltpu.SemaphoreType.DMA((count,)),
            pltpu.SemaphoreType.DMA(()),
        ],
        compiler_params=pltpu.CompilerParams(vmem_limit_bytes=16 << 20),
        name="spectra",
    )(
        pltpu.with_memory_space_constraint(images, pltpu.HBM),
        pltpu.with_memory_space_constraint(table, pltpu.HBM),
    )


def gram_kernel(x_ref, own_ref, send_ref, gram_ref):
    core = lax.rem(lax.axis_index("grp"), 2)
    x = x_ref[...]
    rows, radii = x.shape
    wide = x.astype(jnp.float32).reshape(rows // 8, 8, radii)
    turned = pltpu.roll(wide, 4, 1)
    spot = lax.broadcasted_iota(jnp.int32, turned.shape, 1)
    turned = jnp.where(spot < 4, -turned, turned).reshape(rows, radii).astype(jnp.bfloat16)
    dims = (((0,), (0,)), ((), ()))
    gram_ref[:, :radii] = lax.dot_general(x, x, dims, preferred_element_type=jnp.float32)
    gram_ref[:, radii:] = lax.dot_general(x, turned, dims, preferred_element_type=jnp.float32)
    part = own_ref.shape[1]
    for top in range(2):
        mine = pl.multiple_of((2 * top + core) * part, 8)
        other = pl.multiple_of((2 * top + 1 - core) * part, 8)
        own_ref[top] = gram_ref[pl.ds(mine, part), :]
        send_ref[top] = gram_ref[pl.ds(other, part), :]


def gram_call(pooled):
    rows, radii = pooled.shape
    half = jax.ShapeDtypeStruct((2, radii // 4, 2 * radii), jnp.float32)
    return pl.pallas_call(
        gram_kernel,
        out_shape=(half, half),
        scratch_shapes=[pltpu.VMEM((radii, 2 * radii), jnp.float32)],
        compiler_params=pltpu.CompilerParams(vmem_limit_bytes=8 << 20),
        name="gram",
    )(pooled)


def merge_kernel(scale, own_ref, got_ref, out_ref, rows_ref):
    radii = own_ref.shape[2] // 2
    part = own_ref.shape[1]
    for top in range(2):
        for half in range(2):
            for kind in range(2):
                cols = slice(kind * radii + half * LANES, kind * radii + (half + 1) * LANES)
                total = (own_ref[top, :, cols] + got_ref[top, :, cols]) * scale
                first = (top * 2 + half) * part * 2 + kind
                rows_ref[pl.ds(first, part, stride=2), :] = total
    out_ref[...] = rows_ref[...].astype(jnp.bfloat16)


def merge_call(own, got, total_img):
    rows = own.size // LANES
    return pl.pallas_call(
        functools.partial(merge_kernel, 1.0 / total_img),
        out_shape=jax.ShapeDtypeStruct((rows, LANES), jnp.bfloat16),
        scratch_shapes=[pltpu.VMEM((rows, LANES), jnp.float32)],
        compiler_params=pltpu.CompilerParams(vmem_limit_bytes=8 << 20),
        name="merge",
    )(own, got)


def legendre_kernel(corr_ref, real_ref, imag_ref, out_ref, rows_ref):
    rows_ref[...] = corr_ref[...].astype(jnp.float32)
    harms = real_ref.shape[1]

    def summed(kind):
        low = rows_ref[pl.ds(kind, harms, stride=2), :]
        return low + rows_ref[pl.ds(2 * harms + kind, harms, stride=2), :]

    exact = functools.partial(
        jnp.dot, precision=lax.Precision.HIGHEST, preferred_element_type=jnp.float32
    )
    out_ref[...] = exact(real_ref[...], summed(0)) + exact(imag_ref[...], summed(1))


def legendre_call(corr, legendre_real, legendre_imag):
    degrees = legendre_real.shape[0]
    return pl.pallas_call(
        legendre_kernel,
        out_shape=jax.ShapeDtypeStruct((degrees, LANES), jnp.float32),
        scratch_shapes=[pltpu.VMEM(corr.shape, jnp.float32)],
        compiler_params=pltpu.CompilerParams(vmem_limit_bytes=8 << 20),
        name="legendre",
    )(corr, legendre_real, legendre_imag)


def project_kernel(inv_ref, amp_ref, out_ref):
    part = inv_ref.shape[0] // 2
    exact = functools.partial(
        jnp.dot, precision=lax.Precision.HIGHEST, preferred_element_type=jnp.float32
    )
    low = exact(inv_ref[:part, :], amp_ref[0, :LANES, :])
    out_ref[0] = low + exact(inv_ref[part:, :], amp_ref[0, LANES:, :])


def project_call(inverted, amplitudes):
    return pl.pallas_call(
        project_kernel,
        out_shape=jax.ShapeDtypeStruct(
            (1, inverted.shape[0] // 2, amplitudes.shape[2]), jnp.float32
        ),
        compiler_params=pltpu.CompilerParams(vmem_limit_bytes=8 << 20),
        name="project",
    )(inverted, amplitudes)


def body(images, legendre_real, legendre_imag, amplitudes):
    local_img, radii, points = images.shape
    groups = lax.axis_size("grp")
    owners = lax.axis_size("wide")
    total_img = local_img * groups * owners

    spectra = spectra_call(images, jnp.asarray(table_rows(points, HARMS)))
    spectra = spectra.reshape(HARMS, 2 * local_img, radii)
    pooled = lax.all_to_all(spectra, "wide", split_axis=0, concat_axis=0, tiled=True)

    own, send = gram_call(pooled.reshape(HARMS * 2 * local_img, radii))
    swap = [(g * owners + w, (g ^ 1) * owners + w) for g in range(groups) for w in range(owners)]
    got = lax.ppermute(send, ("grp", "wide"), swap)
    corr = merge_call(own, got, total_img)

    columns = [
        [(2 * top + core) * owners + w for top in range(2) for w in range(owners)]
        for core in range(2)
    ]
    every_harm = lax.all_to_all(
        corr.reshape(2 * owners, 2, LANES), ("grp", "wide"), split_axis=0, concat_axis=0,
        axis_index_groups=columns, tiled=True,
    )
    degree_part = legendre_call(
        every_harm.reshape(4 * owners, LANES), legendre_real, legendre_imag
    )
    mine = lax.all_to_all(
        degree_part.reshape(owners, 1, LANES), "wide", split_axis=0, concat_axis=0, tiled=True
    )
    return project_call(mine.reshape(owners, LANES), amplitudes)


def solution(mesh):
    return jax.shard_map(
        body,
        mesh=mesh,
        in_specs=(P(("grp", "wide"), None, None), P(), P(), P("wide", None, None)),
        out_specs=P("wide", "grp", None),
        check_vma=False,
    )
```

```python
import functools
import math

import jax
import jax.numpy as jnp
import ml_dtypes
import numpy as np
from jax import lax
from jax.experimental import pallas as pl
from jax.experimental.pallas import tpu as pltpu
from jax.sharding import PartitionSpec as P

HARMS = 128
LANES = 128


def table_rows(points, count):
    product = np.arange(count)[:, None] * np.arange(points)[None, :] % points
    phase = product.astype(np.float32) * np.float32(2.0 * math.pi / points)
    norm_scale = np.float32(1.0 / math.sqrt(points))
    both = np.concatenate([np.cos(phase) * norm_scale, -np.sin(phase) * norm_scale])
    return both.astype(ml_dtypes.bfloat16)


def skewed_order():
    return [
        ((z + x + y) % 4 * 4 + (x + y) % 4) * 8 + y
        for z in range(4) for x in range(4) for y in range(8)
    ]


def spectra_kernel(img_hbm, table_hbm, out_ref, img_ref, table_ref, rows_ref, img_sem, table_sem):
    count = img_ref.shape[0]
    harms = table_ref.shape[0] // 2
    table_copy = pltpu.make_async_copy(table_hbm, table_ref, table_sem)
    table_copy.start()

    def image_copy(i):
        return pltpu.make_async_copy(img_hbm.at[i], img_ref.at[i], img_sem.at[i])

    @pl.loop(0, count)
    def _(i):
        image_copy(i).start()

    table_copy.wait()

    @pl.loop(0, count // 2)
    def _(pair):
        image_copy(2 * pair).wait()
        image_copy(2 * pair + 1).wait()
        both = lax.dot_general(
            table_ref[...],
            img_ref[pl.ds(2 * pair, 2)].reshape(-1, img_ref.shape[2]),
            (((1,), (1,)), ((), ())),
            preferred_element_type=jnp.float32,
        )
        halves = rows_ref.shape[0]
        for part in range(2 * halves):
            i = 2 * pair + part // halves
            half = part % halves
            cols = slice(part * LANES, (part + 1) * LANES)
            rows_ref[half, pl.ds(i, harms, stride=8), :] = both[:harms, cols]
            rows_ref[half, pl.ds(i + 4, harms, stride=8), :] = both[harms:, cols]

    for half in range(rows_ref.shape[0]):
        out_ref[:, half * LANES:(half + 1) * LANES] = rows_ref[half].astype(jnp.bfloat16)


def spectra_call(images, table):
    count, radii, points = images.shape
    wide = table.shape[0]
    rows = wide * count
    return pl.pallas_call(
        spectra_kernel,
        out_shape=jax.ShapeDtypeStruct((rows, radii), jnp.bfloat16),
        in_specs=[pl.BlockSpec(memory_space=pltpu.HBM)] * 2,
        scratch_shapes=[
            pltpu.VMEM(images.shape, jnp.bfloat16),
            pltpu.VMEM(table.shape, jnp.bfloat16),
            pltpu.VMEM((radii // LANES, rows, LANES), jnp.float32),
            pltpu.SemaphoreType.DMA((count,)),
            pltpu.SemaphoreType.DMA(()),
        ],
        compiler_params=pltpu.CompilerParams(vmem_limit_bytes=16 << 20),
        name="spectra",
    )(
        pltpu.with_memory_space_constraint(images, pltpu.HBM),
        pltpu.with_memory_space_constraint(table, pltpu.HBM),
    )


def gram_kernel(x_ref, own_ref, send_ref, gram_ref):
    core = lax.rem(lax.axis_index("grp"), 2)
    x = x_ref[...]
    rows, radii = x.shape
    wide = x.astype(jnp.float32).reshape(rows // 8, 8, radii)
    turned = pltpu.roll(wide, 4, 1)
    spot = lax.broadcasted_iota(jnp.int32, turned.shape, 1)
    turned = jnp.where(spot < 4, -turned, turned).reshape(rows, radii).astype(jnp.bfloat16)
    dims = (((0,), (0,)), ((), ()))
    gram_ref[:, :radii] = lax.dot_general(x, x, dims, preferred_element_type=jnp.float32)
    gram_ref[:, radii:] = lax.dot_general(x, turned, dims, preferred_element_type=jnp.float32)
    part = own_ref.shape[1]
    for top in range(2):
        mine = pl.multiple_of((2 * top + core) * part, 8)
        other = pl.multiple_of((2 * top + 1 - core) * part, 8)
        own_ref[top] = gram_ref[pl.ds(mine, part), :]
        send_ref[top] = gram_ref[pl.ds(other, part), :]


def gram_call(pooled):
    rows, radii = pooled.shape
    half = jax.ShapeDtypeStruct((2, radii // 4, 2 * radii), jnp.float32)
    return pl.pallas_call(
        gram_kernel,
        out_shape=(half, half),
        scratch_shapes=[pltpu.VMEM((radii, 2 * radii), jnp.float32)],
        compiler_params=pltpu.CompilerParams(vmem_limit_bytes=8 << 20),
        name="gram",
    )(pooled)


def merge_kernel(scale, own_ref, got_ref, out_ref, rows_ref):
    radii = own_ref.shape[2] // 2
    part = own_ref.shape[1]
    for top in range(2):
        for half in range(2):
            for kind in range(2):
                cols = slice(kind * radii + half * LANES, kind * radii + (half + 1) * LANES)
                total = (own_ref[top, :, cols] + got_ref[top, :, cols]) * scale
                first = (top * 2 + half) * part * 2 + kind
                rows_ref[pl.ds(first, part, stride=2), :] = total
    out_ref[...] = rows_ref[...].astype(jnp.bfloat16)


def merge_call(own, got, total_img):
    rows = own.size // LANES
    return pl.pallas_call(
        functools.partial(merge_kernel, 1.0 / total_img),
        out_shape=jax.ShapeDtypeStruct((rows, LANES), jnp.bfloat16),
        scratch_shapes=[pltpu.VMEM((rows, LANES), jnp.float32)],
        compiler_params=pltpu.CompilerParams(vmem_limit_bytes=8 << 20),
        name="merge",
    )(own, got)


def legendre_kernel(corr_ref, real_ref, imag_ref, out_ref, rows_ref):
    rows_ref[...] = corr_ref[...].astype(jnp.float32)
    harms = real_ref.shape[1]

    def summed(kind):
        low = rows_ref[pl.ds(kind, harms, stride=2), :]
        return low + rows_ref[pl.ds(2 * harms + kind, harms, stride=2), :]

    exact = functools.partial(
        jnp.dot, precision=lax.Precision.HIGHEST, preferred_element_type=jnp.float32
    )
    result = exact(real_ref[...], summed(0)) + exact(imag_ref[...], summed(1))
    tiles = result.reshape(result.shape[0] // 8, 8, LANES)
    spot = lax.broadcasted_iota(jnp.int32, (8, LANES), 0) % 4
    for z in range(4):
        for x in range(4):
            rows = tiles[z * 4 + x]
            for y in range(4):
                rows = jnp.where(spot == y, tiles[(z + x + y) % 4 * 4 + (x + y) % 4], rows)
            out_ref[(z * 4 + x) * 8:(z * 4 + x + 1) * 8, :] = rows


def legendre_call(corr, legendre_real, legendre_imag):
    degrees = legendre_real.shape[0]
    return pl.pallas_call(
        legendre_kernel,
        out_shape=jax.ShapeDtypeStruct((degrees, LANES), jnp.float32),
        scratch_shapes=[pltpu.VMEM(corr.shape, jnp.float32)],
        compiler_params=pltpu.CompilerParams(vmem_limit_bytes=8 << 20),
        name="legendre",
    )(corr, legendre_real, legendre_imag)


def project_kernel(inv_ref, amp_ref, out_ref):
    part = inv_ref.shape[0] // 2
    exact = functools.partial(
        jnp.dot, precision=lax.Precision.HIGHEST, preferred_element_type=jnp.float32
    )
    low = exact(inv_ref[:part, :], amp_ref[0, :LANES, :])
    out_ref[0] = low + exact(inv_ref[part:, :], amp_ref[0, LANES:, :])


def project_call(inverted, amplitudes):
    return pl.pallas_call(
        project_kernel,
        out_shape=jax.ShapeDtypeStruct(
            (1, inverted.shape[0] // 2, amplitudes.shape[2]), jnp.float32
        ),
        compiler_params=pltpu.CompilerParams(vmem_limit_bytes=8 << 20),
        name="project",
    )(inverted, amplitudes)


def body(images, legendre_real, legendre_imag, amplitudes):
    local_img, radii, points = images.shape
    groups = lax.axis_size("grp")
    owners = lax.axis_size("wide")
    total_img = local_img * groups * owners

    spectra = spectra_call(images, jnp.asarray(table_rows(points, HARMS)))
    spectra = spectra.reshape(HARMS, 2 * local_img, radii)
    order = skewed_order()
    rings = [[g * owners + w for w in order] for g in range(groups)]
    pooled = lax.all_to_all(
        spectra, ("grp", "wide"), split_axis=0, concat_axis=0, axis_index_groups=rings, tiled=True
    )

    own, send = gram_call(pooled.reshape(HARMS * 2 * local_img, radii))
    swap = [(g * owners + w, (g ^ 1) * owners + w) for g in range(groups) for w in range(owners)]
    got = lax.ppermute(send, ("grp", "wide"), swap)
    corr = merge_call(own, got, total_img)

    columns = [
        [(2 * top + core) * owners + w for top in range(2) for w in order]
        for core in range(2)
    ]
    every_harm = lax.all_to_all(
        corr.reshape(2 * owners, 2, LANES), ("grp", "wide"), split_axis=0, concat_axis=0,
        axis_index_groups=columns, tiled=True,
    )
    degree_part = legendre_call(
        every_harm.reshape(4 * owners, LANES), legendre_real, legendre_imag
    )
    mine = lax.all_to_all(
        degree_part.reshape(owners, 1, LANES), ("grp", "wide"), split_axis=0, concat_axis=0,
        axis_index_groups=rings, tiled=True,
    )
    return project_call(mine.reshape(owners, LANES), amplitudes)


def solution(mesh):
    return jax.shard_map(
        body,
        mesh=mesh,
        in_specs=(P(("grp", "wide"), None, None), P(), P(), P("wide", None, None)),
        out_specs=P("wide", "grp", None),
        check_vma=False,
    )
```

```python
import functools
import math

import jax
import jax.numpy as jnp
import ml_dtypes
import numpy as np
from jax import lax
from jax.experimental import pallas as pl
from jax.experimental.pallas import tpu as pltpu
from jax.sharding import PartitionSpec as P

HARMS = 128
LANES = 128


def table_rows(points, count):
    product = np.arange(count)[:, None] * np.arange(points)[None, :] % points
    phase = product.astype(np.float32) * np.float32(2.0 * math.pi / points)
    norm_scale = np.float32(1.0 / math.sqrt(points))
    real, imag = np.cos(phase) * norm_scale, -np.sin(phase) * norm_scale
    both = [np.concatenate([real, imag]), np.concatenate([real[::-1], imag[::-1]])]
    return np.stack(both).astype(ml_dtypes.bfloat16)


def skewed_order():
    return [
        ((z + x + y) % 4 * 4 + (x + y) % 4) * 8 + y
        for z in range(4) for x in range(4) for y in range(8)
    ]


def spectra_kernel(img_hbm, table_hbm, out_ref, img_ref, table_ref, rows_ref, img_sem, table_sem):
    count = img_ref.shape[0]
    harms = table_ref.shape[0] // 2
    core = lax.rem(lax.axis_index("grp"), 2)
    table_copy = pltpu.make_async_copy(table_hbm.at[core], table_ref, table_sem)
    table_copy.start()

    def image_copy(i):
        return pltpu.make_async_copy(img_hbm.at[i], img_ref.at[i], img_sem.at[i])

    @pl.loop(0, count)
    def _(i):
        image_copy(i).start()

    table_copy.wait()

    @pl.loop(0, count // 2)
    def _(pair):
        image_copy(2 * pair).wait()
        image_copy(2 * pair + 1).wait()
        both = lax.dot_general(
            table_ref[...],
            img_ref[pl.ds(2 * pair, 2)].reshape(-1, img_ref.shape[2]),
            (((1,), (1,)), ((), ())),
            preferred_element_type=jnp.float32,
        )
        halves = rows_ref.shape[0]
        for part in range(2 * halves):
            i = 2 * pair + part // halves
            half = part % halves
            cols = slice(part * LANES, (part + 1) * LANES)
            rows_ref[half, pl.ds(i, harms, stride=8), :] = both[:harms, cols]
            rows_ref[half, pl.ds(i + 4, harms, stride=8), :] = both[harms:, cols]

    for half in range(rows_ref.shape[0]):
        out_ref[:, half * LANES:(half + 1) * LANES] = rows_ref[half].astype(jnp.bfloat16)


def spectra_call(images, table):
    count, radii, points = images.shape
    wide = table.shape[1]
    rows = wide * count
    return pl.pallas_call(
        spectra_kernel,
        out_shape=jax.ShapeDtypeStruct((rows, radii), jnp.bfloat16),
        in_specs=[pl.BlockSpec(memory_space=pltpu.HBM)] * 2,
        scratch_shapes=[
            pltpu.VMEM(images.shape, jnp.bfloat16),
            pltpu.VMEM(table.shape[1:], jnp.bfloat16),
            pltpu.VMEM((radii // LANES, rows, LANES), jnp.float32),
            pltpu.SemaphoreType.DMA((count,)),
            pltpu.SemaphoreType.DMA(()),
        ],
        compiler_params=pltpu.CompilerParams(vmem_limit_bytes=16 << 20),
        name="spectra",
    )(
        pltpu.with_memory_space_constraint(images, pltpu.HBM),
        pltpu.with_memory_space_constraint(table, pltpu.HBM),
    )


def gram_kernel(x_ref, own_ref, send_ref, gram_ref):
    core = lax.rem(lax.axis_index("grp"), 2)
    x = x_ref[...]
    rows, radii = x.shape
    wide = x.astype(jnp.float32).reshape(rows // 8, 8, radii)
    turned = pltpu.roll(wide, 4, 1)
    spot = lax.broadcasted_iota(jnp.int32, turned.shape, 1)
    turned = jnp.where(spot < 4, -turned, turned).reshape(rows, radii).astype(jnp.bfloat16)
    dims = (((0,), (0,)), ((), ()))
    gram_ref[:, :radii] = lax.dot_general(x, x, dims, preferred_element_type=jnp.float32)
    gram_ref[:, radii:] = lax.dot_general(x, turned, dims, preferred_element_type=jnp.float32)
    part = own_ref.shape[1]
    for top in range(2):
        mine = pl.multiple_of((2 * top + core) * part, 8)
        other = pl.multiple_of((2 * top + 1 - core) * part, 8)
        own_ref[top] = gram_ref[pl.ds(mine, part), :]
        send_ref[top] = gram_ref[pl.ds(other, part), :]


def gram_call(pooled):
    rows, radii = pooled.shape
    half = jax.ShapeDtypeStruct((2, radii // 4, 2 * radii), jnp.float32)
    return pl.pallas_call(
        gram_kernel,
        out_shape=(half, half),
        scratch_shapes=[pltpu.VMEM((radii, 2 * radii), jnp.float32)],
        compiler_params=pltpu.CompilerParams(vmem_limit_bytes=8 << 20),
        name="gram",
    )(pooled)


def merge_kernel(scale, own_ref, got_ref, out_ref, rows_ref):
    radii = own_ref.shape[2] // 2
    part = own_ref.shape[1]
    for top in range(2):
        for half in range(2):
            for kind in range(2):
                cols = slice(kind * radii + half * LANES, kind * radii + (half + 1) * LANES)
                total = (own_ref[top, :, cols] + got_ref[top, :, cols]) * scale
                first = (top * 2 + half) * part * 2 + kind
                rows_ref[pl.ds(first, part, stride=2), :] = total
    out_ref[...] = rows_ref[...].astype(jnp.bfloat16)


def merge_call(own, got, total_img):
    rows = own.size // LANES
    return pl.pallas_call(
        functools.partial(merge_kernel, 1.0 / total_img),
        out_shape=jax.ShapeDtypeStruct((rows, LANES), jnp.bfloat16),
        scratch_shapes=[pltpu.VMEM((rows, LANES), jnp.float32)],
        compiler_params=pltpu.CompilerParams(vmem_limit_bytes=8 << 20),
        name="merge",
    )(own, got)


def legendre_kernel(corr_ref, real_ref, imag_ref, out_ref, rows_ref):
    rows_ref[...] = corr_ref[...].astype(jnp.float32)
    harms = real_ref.shape[1]

    def summed(kind):
        low = rows_ref[pl.ds(kind, harms, stride=2), :]
        return low + rows_ref[pl.ds(2 * harms + kind, harms, stride=2), :]

    exact = functools.partial(
        jnp.dot, precision=lax.Precision.HIGHEST, preferred_element_type=jnp.float32
    )
    result = exact(real_ref[...], summed(0)) + exact(imag_ref[...], summed(1))
    tiles = result.reshape(result.shape[0] // 8, 8, LANES)
    spot = lax.broadcasted_iota(jnp.int32, (8, LANES), 0) % 4
    for z in range(4):
        for x in range(4):
            rows = tiles[z * 4 + x]
            for y in range(4):
                rows = jnp.where(spot == y, tiles[(z + x + y) % 4 * 4 + (x + y) % 4], rows)
            out_ref[(z * 4 + x) * 8:(z * 4 + x + 1) * 8, :] = rows


def legendre_call(corr, legendre_real, legendre_imag):
    degrees = legendre_real.shape[0]
    return pl.pallas_call(
        legendre_kernel,
        out_shape=jax.ShapeDtypeStruct((degrees, LANES), jnp.float32),
        scratch_shapes=[pltpu.VMEM(corr.shape, jnp.float32)],
        compiler_params=pltpu.CompilerParams(vmem_limit_bytes=8 << 20),
        name="legendre",
    )(corr, legendre_real, legendre_imag)


def project_kernel(inv_ref, amp_ref, out_ref):
    part = inv_ref.shape[0] // 2
    exact = functools.partial(
        jnp.dot, precision=lax.Precision.HIGHEST, preferred_element_type=jnp.float32
    )
    low = exact(inv_ref[:part, :], amp_ref[0, :LANES, :])
    out_ref[0] = low + exact(inv_ref[part:, :], amp_ref[0, LANES:, :])


def project_call(inverted, amplitudes):
    return pl.pallas_call(
        project_kernel,
        out_shape=jax.ShapeDtypeStruct(
            (1, inverted.shape[0] // 2, amplitudes.shape[2]), jnp.float32
        ),
        compiler_params=pltpu.CompilerParams(vmem_limit_bytes=8 << 20),
        name="project",
    )(inverted, amplitudes)


def body(images, legendre_real, legendre_imag, amplitudes):
    local_img, radii, points = images.shape
    groups = lax.axis_size("grp")
    owners = lax.axis_size("wide")
    total_img = local_img * groups * owners

    spectra = spectra_call(images, jnp.asarray(table_rows(points, HARMS)))
    spectra = spectra.reshape(HARMS, 2 * local_img, radii)
    order = skewed_order()
    rings = [[g * owners + w for w in order] for g in range(groups)]
    both_ways = [ring[::-1] if g % 2 else ring for g, ring in enumerate(rings)]
    pooled = lax.all_to_all(
        spectra, ("grp", "wide"), split_axis=0, concat_axis=0, axis_index_groups=both_ways, tiled=True
    )

    own, send = gram_call(pooled.reshape(HARMS * 2 * local_img, radii))
    swap = [(g * owners + w, (g ^ 1) * owners + w) for g in range(groups) for w in range(owners)]
    got = lax.ppermute(send, ("grp", "wide"), swap)
    corr = merge_call(own, got, total_img)

    columns = [
        [(2 * top + core) * owners + w for top in range(2) for w in order]
        for core in range(2)
    ]
    every_harm = lax.all_to_all(
        corr.reshape(2 * owners, 2, LANES), ("grp", "wide"), split_axis=0, concat_axis=0,
        axis_index_groups=columns, tiled=True,
    )
    degree_part = legendre_call(
        every_harm.reshape(4 * owners, LANES), legendre_real, legendre_imag
    )
    mine = lax.all_to_all(
        degree_part.reshape(owners, 1, LANES), ("grp", "wide"), split_axis=0, concat_axis=0,
        axis_index_groups=rings, tiled=True,
    )
    return project_call(mine.reshape(owners, LANES), amplitudes)


def solution(mesh):
    return jax.shard_map(
        body,
        mesh=mesh,
        in_specs=(P(("grp", "wide"), None, None), P(), P(), P("wide", None, None)),
        out_specs=P("wide", "grp", None),
        check_vma=False,
    )
```

```python
import functools
import math

import jax
import jax.numpy as jnp
import ml_dtypes
import numpy as np
from jax import lax
from jax.experimental import pallas as pl
from jax.experimental.pallas import tpu as pltpu
from jax.sharding import PartitionSpec as P

HARMS = 128
LANES = 128


def table_rows(points, count):
    product = np.arange(count)[:, None] * np.arange(points)[None, :] % points
    phase = product.astype(np.float32) * np.float32(2.0 * math.pi / points)
    norm_scale = np.float32(1.0 / math.sqrt(points))
    real, imag = np.cos(phase) * norm_scale, -np.sin(phase) * norm_scale
    both = [np.concatenate([real, imag]), np.concatenate([real[::-1], imag[::-1]])]
    return np.stack(both).astype(ml_dtypes.bfloat16)


def spectra_kernel(img_hbm, table_hbm, out_ref, img_ref, table_ref, rows_ref, img_sem, table_sem):
    count = img_ref.shape[0]
    harms = table_ref.shape[0] // 2
    core = lax.rem(lax.axis_index("grp"), 2)
    table_copy = pltpu.make_async_copy(table_hbm.at[core], table_ref, table_sem)
    table_copy.start()

    def image_copy(i):
        return pltpu.make_async_copy(img_hbm.at[i], img_ref.at[i], img_sem.at[i])

    @pl.loop(0, count)
    def _(i):
        image_copy(i).start()

    table_copy.wait()

    @pl.loop(0, count // 2)
    def _(pair):
        image_copy(2 * pair).wait()
        image_copy(2 * pair + 1).wait()
        both = lax.dot_general(
            table_ref[...],
            img_ref[pl.ds(2 * pair, 2)].reshape(-1, img_ref.shape[2]),
            (((1,), (1,)), ((), ())),
            preferred_element_type=jnp.float32,
        )
        halves = rows_ref.shape[0]
        for part in range(2 * halves):
            i = 2 * pair + part // halves
            half = part % halves
            cols = slice(part * LANES, (part + 1) * LANES)
            rows_ref[half, pl.ds(i, harms, stride=8), :] = both[:harms, cols]
            rows_ref[half, pl.ds(i + 4, harms, stride=8), :] = both[harms:, cols]

    for half in range(rows_ref.shape[0]):
        out_ref[:, half * LANES:(half + 1) * LANES] = rows_ref[half].astype(jnp.bfloat16)


def spectra_call(images, table):
    count, radii, points = images.shape
    wide = table.shape[1]
    rows = wide * count
    return pl.pallas_call(
        spectra_kernel,
        out_shape=jax.ShapeDtypeStruct((rows, radii), jnp.bfloat16),
        in_specs=[pl.BlockSpec(memory_space=pltpu.HBM)] * 2,
        scratch_shapes=[
            pltpu.VMEM(images.shape, jnp.bfloat16),
            pltpu.VMEM(table.shape[1:], jnp.bfloat16),
            pltpu.VMEM((radii // LANES, rows, LANES), jnp.float32),
            pltpu.SemaphoreType.DMA((count,)),
            pltpu.SemaphoreType.DMA(()),
        ],
        compiler_params=pltpu.CompilerParams(vmem_limit_bytes=16 << 20),
        name="spectra",
    )(
        pltpu.with_memory_space_constraint(images, pltpu.HBM),
        pltpu.with_memory_space_constraint(table, pltpu.HBM),
    )


def gram_kernel(x_ref, own_ref, send_ref, gram_ref):
    core = lax.rem(lax.axis_index("grp"), 2)
    x = x_ref[...]
    rows, radii = x.shape
    wide = x.astype(jnp.float32).reshape(rows // 8, 8, radii)
    turned = pltpu.roll(wide, 4, 1)
    spot = lax.broadcasted_iota(jnp.int32, turned.shape, 1)
    turned = jnp.where(spot < 4, -turned, turned).reshape(rows, radii).astype(jnp.bfloat16)
    dims = (((0,), (0,)), ((), ()))
    gram_ref[:, :radii] = lax.dot_general(x, x, dims, preferred_element_type=jnp.float32)
    gram_ref[:, radii:] = lax.dot_general(x, turned, dims, preferred_element_type=jnp.float32)
    part = own_ref.shape[1]
    for top in range(2):
        mine = pl.multiple_of((2 * top + core) * part, 8)
        other = pl.multiple_of((2 * top + 1 - core) * part, 8)
        own_ref[top] = gram_ref[pl.ds(mine, part), :]
        send_ref[top] = gram_ref[pl.ds(other, part), :]


def gram_call(pooled):
    rows, radii = pooled.shape
    half = jax.ShapeDtypeStruct((2, radii // 4, 2 * radii), jnp.float32)
    return pl.pallas_call(
        gram_kernel,
        out_shape=(half, half),
        scratch_shapes=[pltpu.VMEM((radii, 2 * radii), jnp.float32)],
        compiler_params=pltpu.CompilerParams(vmem_limit_bytes=8 << 20),
        name="gram",
    )(pooled)


def merge_kernel(scale, own_ref, got_ref, out_ref, rows_ref):
    radii = own_ref.shape[2] // 2
    part = own_ref.shape[1]
    for top in range(2):
        for half in range(2):
            for kind in range(2):
                cols = slice(kind * radii + half * LANES, kind * radii + (half + 1) * LANES)
                total = (own_ref[top, :, cols] + got_ref[top, :, cols]) * scale
                first = (top * 2 + half) * part * 2 + kind
                rows_ref[pl.ds(first, part, stride=2), :] = total
    out_ref[...] = rows_ref[...].astype(jnp.bfloat16)


def merge_call(own, got, total_img):
    rows = own.size // LANES
    return pl.pallas_call(
        functools.partial(merge_kernel, 1.0 / total_img),
        out_shape=jax.ShapeDtypeStruct((rows, LANES), jnp.bfloat16),
        scratch_shapes=[pltpu.VMEM((rows, LANES), jnp.float32)],
        compiler_params=pltpu.CompilerParams(vmem_limit_bytes=8 << 20),
        name="merge",
    )(own, got)


def legendre_kernel(corr_ref, real_ref, imag_ref, out_ref, rows_ref):
    rows_ref[...] = corr_ref[...].astype(jnp.float32)
    harms = real_ref.shape[1]

    def summed(kind):
        low = rows_ref[pl.ds(kind, harms, stride=2), :]
        return low + rows_ref[pl.ds(2 * harms + kind, harms, stride=2), :]

    exact = functools.partial(
        jnp.dot, precision=lax.Precision.HIGHEST, preferred_element_type=jnp.float32
    )
    out_ref[...] = exact(real_ref[...], summed(0)) + exact(imag_ref[...], summed(1))


def legendre_call(corr, legendre_real, legendre_imag):
    degrees = legendre_real.shape[0]
    return pl.pallas_call(
        legendre_kernel,
        out_shape=jax.ShapeDtypeStruct((degrees, LANES), jnp.float32),
        scratch_shapes=[pltpu.VMEM(corr.shape, jnp.float32)],
        compiler_params=pltpu.CompilerParams(vmem_limit_bytes=8 << 20),
        name="legendre",
    )(corr, legendre_real, legendre_imag)


def project_kernel(inv_ref, amp_ref, out_ref):
    part = inv_ref.shape[0] // 2
    exact = functools.partial(
        jnp.dot, precision=lax.Precision.HIGHEST, preferred_element_type=jnp.float32
    )
    low = exact(inv_ref[:part, :], amp_ref[0, :LANES, :])
    out_ref[0] = low + exact(inv_ref[part:, :], amp_ref[0, LANES:, :])


def project_call(inverted, amplitudes):
    return pl.pallas_call(
        project_kernel,
        out_shape=jax.ShapeDtypeStruct(
            (1, inverted.shape[0] // 2, amplitudes.shape[2]), jnp.float32
        ),
        compiler_params=pltpu.CompilerParams(vmem_limit_bytes=8 << 20),
        name="project",
    )(inverted, amplitudes)


def body(images, legendre_real, legendre_imag, amplitudes):
    local_img, radii, points = images.shape
    groups = lax.axis_size("grp")
    owners = lax.axis_size("wide")
    total_img = local_img * groups * owners

    spectra = spectra_call(images, jnp.asarray(table_rows(points, HARMS)))
    spectra = spectra.reshape(HARMS, 2 * local_img, radii)
    rings = [[g * owners + w for w in range(owners)] for g in range(groups)]
    both_ways = [ring[::-1] if g % 2 else ring for g, ring in enumerate(rings)]
    pooled = lax.all_to_all(
        spectra, ("grp", "wide"), split_axis=0, concat_axis=0, axis_index_groups=both_ways, tiled=True
    )

    own, send = gram_call(pooled.reshape(HARMS * 2 * local_img, radii))
    swap = [(g * owners + w, (g ^ 1) * owners + w) for g in range(groups) for w in range(owners)]
    got = lax.ppermute(send, ("grp", "wide"), swap)
    corr = merge_call(own, got, total_img)

    columns = [
        [(2 * top + core) * owners + w for top in range(2) for w in range(owners)]
        for core in range(2)
    ]
    every_harm = lax.all_to_all(
        corr.reshape(2 * owners, 2, LANES), ("grp", "wide"), split_axis=0, concat_axis=0,
        axis_index_groups=columns, tiled=True,
    )
    degree_part = legendre_call(
        every_harm.reshape(4 * owners, LANES), legendre_real, legendre_imag
    )
    mine = lax.all_to_all(
        degree_part.reshape(owners, 1, LANES), ("grp", "wide"), split_axis=0, concat_axis=0,
        axis_index_groups=rings, tiled=True,
    )
    return project_call(mine.reshape(owners, LANES), amplitudes)


def solution(mesh):
    return jax.shard_map(
        body,
        mesh=mesh,
        in_specs=(P(("grp", "wide"), None, None), P(), P(), P("wide", None, None)),
        out_specs=P("wide", "grp", None),
        check_vma=False,
    )
```

```python
import functools
import math

import jax
import jax.numpy as jnp
import ml_dtypes
import numpy as np
from jax import lax
from jax.experimental import pallas as pl
from jax.experimental.pallas import tpu as pltpu
from jax.sharding import PartitionSpec as P

HARMS = 128
LANES = 128


def table_rows(points, count):
    product = np.arange(count)[:, None] * np.arange(points)[None, :] % points
    phase = product.astype(np.float32) * np.float32(2.0 * math.pi / points)
    norm_scale = np.float32(1.0 / math.sqrt(points))
    real, imag = np.cos(phase) * norm_scale, -np.sin(phase) * norm_scale
    both = [np.concatenate([real[::-1], imag[::-1]]), np.concatenate([real, imag])]
    return np.stack(both).astype(ml_dtypes.bfloat16)


def spectra_kernel(img_hbm, table_hbm, out_ref, img_ref, table_ref, rows_ref, img_sem, table_sem):
    count = img_ref.shape[0]
    harms = table_ref.shape[0] // 2
    core = lax.rem(lax.axis_index("grp"), 2)
    table_copy = pltpu.make_async_copy(table_hbm.at[core], table_ref, table_sem)
    table_copy.start()

    def image_copy(i):
        return pltpu.make_async_copy(img_hbm.at[i], img_ref.at[i], img_sem.at[i])

    @pl.loop(0, count)
    def _(i):
        image_copy(i).start()

    table_copy.wait()

    @pl.loop(0, count // 2)
    def _(pair):
        image_copy(2 * pair).wait()
        image_copy(2 * pair + 1).wait()
        both = lax.dot_general(
            table_ref[...],
            img_ref[pl.ds(2 * pair, 2)].reshape(-1, img_ref.shape[2]),
            (((1,), (1,)), ((), ())),
            preferred_element_type=jnp.float32,
        )
        halves = rows_ref.shape[0]
        for part in range(2 * halves):
            i = 2 * pair + part // halves
            half = part % halves
            cols = slice(part * LANES, (part + 1) * LANES)
            rows_ref[half, pl.ds(i, harms, stride=8), :] = both[:harms, cols]
            rows_ref[half, pl.ds(i + 4, harms, stride=8), :] = both[harms:, cols]

    for half in range(rows_ref.shape[0]):
        out_ref[:, half * LANES:(half + 1) * LANES] = rows_ref[half].astype(jnp.bfloat16)


def spectra_call(images, table):
    count, radii, points = images.shape
    wide = table.shape[1]
    rows = wide * count
    return pl.pallas_call(
        spectra_kernel,
        out_shape=jax.ShapeDtypeStruct((rows, radii), jnp.bfloat16),
        in_specs=[pl.BlockSpec(memory_space=pltpu.HBM)] * 2,
        scratch_shapes=[
            pltpu.VMEM(images.shape, jnp.bfloat16),
            pltpu.VMEM(table.shape[1:], jnp.bfloat16),
            pltpu.VMEM((radii // LANES, rows, LANES), jnp.float32),
            pltpu.SemaphoreType.DMA((count,)),
            pltpu.SemaphoreType.DMA(()),
        ],
        compiler_params=pltpu.CompilerParams(vmem_limit_bytes=16 << 20),
        name="spectra",
    )(
        pltpu.with_memory_space_constraint(images, pltpu.HBM),
        pltpu.with_memory_space_constraint(table, pltpu.HBM),
    )


def gram_kernel(x_ref, own_ref, send_ref, gram_ref):
    core = lax.rem(lax.axis_index("grp"), 2)
    x = x_ref[...]
    rows, radii = x.shape
    wide = x.astype(jnp.float32).reshape(rows // 8, 8, radii)
    turned = pltpu.roll(wide, 4, 1)
    spot = lax.broadcasted_iota(jnp.int32, turned.shape, 1)
    turned = jnp.where(spot < 4, -turned, turned).reshape(rows, radii).astype(jnp.bfloat16)
    dims = (((0,), (0,)), ((), ()))
    gram_ref[:, :radii] = lax.dot_general(x, x, dims, preferred_element_type=jnp.float32)
    gram_ref[:, radii:] = lax.dot_general(x, turned, dims, preferred_element_type=jnp.float32)
    part = own_ref.shape[1]
    for top in range(2):
        mine = pl.multiple_of((2 * top + core) * part, 8)
        other = pl.multiple_of((2 * top + 1 - core) * part, 8)
        own_ref[top] = gram_ref[pl.ds(mine, part), :]
        send_ref[top] = gram_ref[pl.ds(other, part), :]


def gram_call(pooled):
    rows, radii = pooled.shape
    half = jax.ShapeDtypeStruct((2, radii // 4, 2 * radii), jnp.float32)
    return pl.pallas_call(
        gram_kernel,
        out_shape=(half, half),
        scratch_shapes=[pltpu.VMEM((radii, 2 * radii), jnp.float32)],
        compiler_params=pltpu.CompilerParams(vmem_limit_bytes=8 << 20),
        name="gram",
    )(pooled)


def merge_kernel(scale, own_ref, got_ref, out_ref, rows_ref):
    radii = own_ref.shape[2] // 2
    part = own_ref.shape[1]
    for top in range(2):
        for half in range(2):
            for kind in range(2):
                cols = slice(kind * radii + half * LANES, kind * radii + (half + 1) * LANES)
                total = (own_ref[top, :, cols] + got_ref[top, :, cols]) * scale
                first = (top * 2 + half) * part * 2 + kind
                rows_ref[pl.ds(first, part, stride=2), :] = total
    out_ref[...] = rows_ref[...].astype(jnp.bfloat16)


def merge_call(own, got, total_img):
    rows = own.size // LANES
    return pl.pallas_call(
        functools.partial(merge_kernel, 1.0 / total_img),
        out_shape=jax.ShapeDtypeStruct((rows, LANES), jnp.bfloat16),
        scratch_shapes=[pltpu.VMEM((rows, LANES), jnp.float32)],
        compiler_params=pltpu.CompilerParams(vmem_limit_bytes=8 << 20),
        name="merge",
    )(own, got)


def legendre_kernel(corr_ref, real_ref, imag_ref, out_ref, rows_ref):
    rows_ref[...] = corr_ref[...].astype(jnp.float32)
    harms = real_ref.shape[1]

    def summed(kind):
        low = rows_ref[pl.ds(kind, harms, stride=2), :]
        return low + rows_ref[pl.ds(2 * harms + kind, harms, stride=2), :]

    exact = functools.partial(
        jnp.dot, precision=lax.Precision.HIGHEST, preferred_element_type=jnp.float32
    )
    out_ref[...] = exact(real_ref[...], summed(0)) + exact(imag_ref[...], summed(1))


def legendre_call(corr, legendre_real, legendre_imag):
    degrees = legendre_real.shape[0]
    return pl.pallas_call(
        legendre_kernel,
        out_shape=jax.ShapeDtypeStruct((degrees, LANES), jnp.float32),
        scratch_shapes=[pltpu.VMEM(corr.shape, jnp.float32)],
        compiler_params=pltpu.CompilerParams(vmem_limit_bytes=8 << 20),
        name="legendre",
    )(corr, legendre_real, legendre_imag)


def project_kernel(inv_ref, amp_ref, out_ref):
    part = inv_ref.shape[0] // 2
    exact = functools.partial(
        jnp.dot, precision=lax.Precision.HIGHEST, preferred_element_type=jnp.float32
    )
    low = exact(inv_ref[:part, :], amp_ref[0, :LANES, :])
    out_ref[0] = low + exact(inv_ref[part:, :], amp_ref[0, LANES:, :])


def project_call(inverted, amplitudes):
    return pl.pallas_call(
        project_kernel,
        out_shape=jax.ShapeDtypeStruct(
            (1, inverted.shape[0] // 2, amplitudes.shape[2]), jnp.float32
        ),
        compiler_params=pltpu.CompilerParams(vmem_limit_bytes=8 << 20),
        name="project",
    )(inverted, amplitudes)


def body(images, legendre_real, legendre_imag, amplitudes):
    local_img, radii, points = images.shape
    groups = lax.axis_size("grp")
    owners = lax.axis_size("wide")
    total_img = local_img * groups * owners

    spectra = spectra_call(images, jnp.asarray(table_rows(points, HARMS)))
    spectra = spectra.reshape(HARMS, 2 * local_img, radii)
    rings = [[g * owners + w for w in range(owners)] for g in range(groups)]
    both_ways = [ring if g % 2 else ring[::-1] for g, ring in enumerate(rings)]
    pooled = lax.all_to_all(
        spectra, ("grp", "wide"), split_axis=0, concat_axis=0, axis_index_groups=both_ways, tiled=True
    )

    own, send = gram_call(pooled.reshape(HARMS * 2 * local_img, radii))
    swap = [(g * owners + w, (g ^ 1) * owners + w) for g in range(groups) for w in range(owners)]
    got = lax.ppermute(send, ("grp", "wide"), swap)
    corr = merge_call(own, got, total_img)

    columns = [
        [(2 * top + core) * owners + w for top in range(2) for w in range(owners)]
        for core in range(2)
    ]
    every_harm = lax.all_to_all(
        corr.reshape(2 * owners, 2, LANES), ("grp", "wide"), split_axis=0, concat_axis=0,
        axis_index_groups=columns, tiled=True,
    )
    degree_part = legendre_call(
        every_harm.reshape(4 * owners, LANES), legendre_real, legendre_imag
    )
    mine = lax.all_to_all(
        degree_part.reshape(owners, 1, LANES), ("grp", "wide"), split_axis=0, concat_axis=0,
        axis_index_groups=rings, tiled=True,
    )
    return project_call(mine.reshape(owners, LANES), amplitudes)


def solution(mesh):
    return jax.shard_map(
        body,
        mesh=mesh,
        in_specs=(P(("grp", "wide"), None, None), P(), P(), P("wide", None, None)),
        out_specs=P("wide", "grp", None),
        check_vma=False,
    )
```
